32 devices in a mesh: seq: 4 (over x, core), dp: 8 (over z, y).
Axes of the slice: x: 2, y: 2, z: 4, core: 2. Of those that a mesh axis runs over, the one named last changes fastest.
Arguments:
- tokens: bfloat16 [8, 2048, 2048], P('dp', 'seq'), may hold values from -6 to 6
- log_decay: float32 [8, 8, 2048], P('dp', None, 'seq'), may hold values from -1 to 0
- w_qkv: bfloat16 [2048, 3072], P('dp'), may hold values from -0.125 to 0.125
- w_gate: bfloat16 [2048, 1024], P('dp'), may hold values from -0.125 to 0.125
- w_out: bfloat16 [1024, 2048], P('dp'), may hold values from -0.1875 to 0.1875
- norm_gain: float32 [1024], replicated, may hold values from 0.1 to 1.9
Outputs:
- mixed_rows: bfloat16 [8, 2048, 2048], P('dp', 'seq')
The draws below stay inside these ranges and needn't reach their ends.
All inputs are finite; a program needn't handle non-finite values.
Results may differ from the reference program's by a relative error of at most 0.0065.
Values may be sent and summed in bfloat16 or wider, within the bound.
A program may use at most 64 MiB of HBM per device.

```python
import math
import jax
import jax.numpy as jnp
from jax import lax

D = 2048
HEAD_TOTAL = 8
HEAD_DIM = 128
TOK_DEV = 512
SEQUENCE_LENGTH = 2048
SEQUENCE_TOTAL = 8
N_SEQ = 4


def draw_log_decay(key, part):
    key_vectors = jax.random.split(key, 6)
    head_draw = jax.random.uniform(key_vectors[0], (SEQUENCE_TOTAL, HEAD_TOTAL, 1), jnp.float32)
    class_draw = jax.random.uniform(key_vectors[1], (SEQUENCE_TOTAL, HEAD_TOTAL, 1), jnp.float32)
    fast_share = 0.5
    slow_low = math.log(0.05 * math.log(10.0) / SEQUENCE_LENGTH)
    slow_high = math.log(0.4 * math.log(10.0) / SEQUENCE_LENGTH)
    slow_rate = jnp.exp(slow_low + head_draw * (slow_high - slow_low))
    fast_rate = jnp.exp(math.log(1.0 / 50.0) + head_draw * math.log(2.0))
    decay_speed = jnp.where(class_draw < fast_share, fast_rate, slow_rate)
    position_multiplier = jnp.exp(jax.random.uniform(key_vectors[2], (SEQUENCE_TOTAL, HEAD_TOTAL, SEQUENCE_LENGTH), jnp.float32, -0.5, 0.5))
    block_multiplier = jax.random.uniform(key_vectors[3], (SEQUENCE_TOTAL, HEAD_TOTAL, SEQUENCE_LENGTH // TOK_DEV, 1), jnp.float32, 0.5, 1.5)
    block_multiplier = jnp.broadcast_to(block_multiplier, (SEQUENCE_TOTAL, HEAD_TOTAL, SEQUENCE_LENGTH // TOK_DEV, TOK_DEV)).reshape(SEQUENCE_TOTAL, HEAD_TOTAL, SEQUENCE_LENGTH)
    spike_sample = jax.random.uniform(key_vectors[4], (SEQUENCE_TOTAL, HEAD_TOTAL, SEQUENCE_LENGTH), jnp.float32)
    spike_penalty = jax.random.uniform(key_vectors[5], (SEQUENCE_TOTAL, HEAD_TOTAL, SEQUENCE_LENGTH), jnp.float32, math.log(0.5), math.log(0.8))
    spike_events = jnp.where(spike_sample < 2.0 / SEQUENCE_LENGTH, spike_penalty, 0.0)
    return (-decay_speed * position_multiplier * block_multiplier + spike_events).astype(jnp.float32)


def block_levels(stream_key, dims, pieces, smallest, high):
    loudness, own = 1.0, jax.random.fold_in(stream_key, 6)
    for position, blocks in pieces:
        steps = jnp.exp(jax.random.uniform(jax.random.fold_in(own, position), (blocks,), jnp.float32, smallest / len(pieces), high / len(pieces)))
        loudness = loudness * jnp.repeat(steps, dims[position] // blocks).reshape([-1 if axis == position else 1 for axis in range(len(dims))])
    return loudness


def noise(key, shape, deviation, limit, shards=(), kind=jnp.bfloat16):
    drawn = deviation * jax.random.normal(key, shape, jnp.float32)
    if shards:
        drawn = drawn * block_levels(key, shape, shards, -0.22, 0.18)
    return jnp.clip(drawn, -limit, limit).astype(kind)


def setup_inputs(seed: int = 0) -> dict:
    keys = jax.random.split(jax.random.key(seed), 7)
    return {
        "tokens": noise(keys[0], (SEQUENCE_TOTAL, SEQUENCE_LENGTH, D), 1.0, 6.0, ((0, 8), (1, 4))),
        "log_decay": draw_log_decay(jax.random.fold_in(keys[6], 71), 0),
        "w_qkv": noise(keys[2], (D, 3 * HEAD_TOTAL * HEAD_DIM), D ** -0.5, 0.125, ((0, 8),)),
        "w_gate": noise(keys[3], (D, HEAD_TOTAL * HEAD_DIM), D ** -0.5, 0.125, ((0, 8),)),
        "w_out": noise(keys[4], (HEAD_TOTAL * HEAD_DIM, D), (HEAD_TOTAL * HEAD_DIM) ** -0.5, 0.1875, ((0, 8),)),
        "norm_gain": jnp.clip(1.0 + 0.18 * jax.random.normal(keys[5], (HEAD_TOTAL * HEAD_DIM,), jnp.float32), 0.1, 1.9),
    }


def block_pass(tok_rows, decay_rows, carried, w_qkv, w_gate, w_out, norm_gain):
    tok_count = tok_rows.shape[0]
    projected = jnp.dot(tok_rows, w_qkv, preferred_element_type=jnp.float32)
    gate_pre = jnp.dot(tok_rows, w_gate, preferred_element_type=jnp.float32)
    activated = jax.nn.silu(projected).astype(jnp.bfloat16).reshape(tok_count, 3, HEAD_TOTAL, HEAD_DIM)
    query_rows = activated[:, 0].astype(jnp.float32)
    key_rows = activated[:, 1].astype(jnp.float32)
    value_rows = activated[:, 2].astype(jnp.float32)
    cum_decay = jnp.cumsum(decay_rows, axis=1)
    block_decay = cum_decay[:, -1]
    scores = jnp.einsum('thd,shd->hts', query_rows, key_rows)
    positions = jnp.arange(tok_count, dtype=jnp.int32)
    causal_mask = (positions[None, :] <= positions[:, None])[None, :, :]
    decay_gap = cum_decay[:, :, None] - cum_decay[:, None, :]
    decay_mat = jnp.where(causal_mask, jnp.exp(jnp.where(causal_mask, decay_gap, 0.0)), 0.0)
    weighted = (scores * decay_mat).astype(jnp.bfloat16)
    intra_part = jnp.einsum('hts,shd->thd', weighted.astype(jnp.float32), value_rows)
    key_factor = jnp.exp(block_decay[:, None] - cum_decay).T
    scaled_key = (key_rows * key_factor[:, :, None]).astype(jnp.bfloat16)
    local_state = jnp.einsum('thd,the->hde', scaled_key.astype(jnp.float32), value_rows)
    query_scaled = query_rows * jnp.exp(cum_decay).T[:, :, None]
    inter_part = jnp.einsum('thd,hde->the', query_scaled, carried, precision=lax.Precision.HIGHEST)
    attended = (intra_part + inter_part).reshape(tok_count, HEAD_TOTAL * HEAD_DIM)
    mean_square = lax.optimization_barrier(jnp.mean(attended * attended, axis=1, keepdims=True))
    normed = attended * lax.rsqrt(mean_square + 1e-06) * norm_gain
    gated = (normed * jax.nn.sigmoid(gate_pre)).astype(jnp.bfloat16)
    mixed_rows = jnp.dot(gated, w_out, preferred_element_type=jnp.float32).astype(jnp.bfloat16)
    new_state = jnp.exp(block_decay)[:, None, None] * carried + local_state
    return (mixed_rows, new_state)

def reference(tokens, log_decay, w_qkv, w_gate, w_out, norm_gain):

    def one_sequence(seq_items):
        seq_rows, seq_decay = seq_items
        blocks = seq_rows.reshape(N_SEQ, TOK_DEV, D)
        decays = seq_decay.reshape(HEAD_TOTAL, N_SEQ, TOK_DEV).transpose(1, 0, 2)

        def advance(carried, block_items):
            mixed_rows, new_state = block_pass(block_items[0], block_items[1], carried, w_qkv, w_gate, w_out, norm_gain)
            return (new_state, mixed_rows)
        first_state = jnp.zeros((HEAD_TOTAL, HEAD_DIM, HEAD_DIM), jnp.float32)
        final_state, outputs = lax.scan(advance, first_state, (blocks, decays))
        return outputs.reshape(SEQUENCE_LENGTH, D)
    return lax.map(one_sequence, (tokens, log_decay))
```

```python
import functools

import jax
import jax.numpy as jnp
from jax import lax
from jax.experimental import pallas as pl
from jax.experimental.pallas import tpu as pltpu
from jax.sharding import PartitionSpec as P

MESH = pl.DeviceIdType.MESH
F32 = jnp.float32
BF16 = jnp.bfloat16


def fused(n_dp, n_seq, tok, ld, gain, wqkv, wgate, wout, out, W, WO, acc, lhs, q_s, k_s, v_s,
          att, ccol, crow, ss, gated, st_local, st_recv, st_send, loc_sem,
          rr, pr, xr, pxr, rs, ps, xs, pxs, ch_s, ch_r):
    T, D = tok.shape
    H = ld.shape[0]
    F = gain.shape[1]
    hd = F // H
    N = n_dp
    s = lax.axis_index("seq")
    d = lax.axis_index("dp")
    core = s % 2
    x = (s // 2) % 2
    partner = s + 1 - 2 * core
    xpeer = s + 2 - 4 * x
    half = N // 2

    def pos_of(i):
        return jnp.where(i % 2 == 0, i // 2, N - 1 - i // 2)

    def dev_at(p):
        p = lax.rem(p + 2 * N, N)
        return jnp.where(p < half, 2 * p, 2 * (N - 1 - p) + 1)

    pos = pos_of(d)
    ring_to = (dev_at(pos + 1), dev_at(pos - 1))

    def origin(dr, k):
        return dev_at(pos - k) if dr == 0 else dev_at(pos + k)

    E = (F + F // 4, 5 * D // 16)
    M = (F + F // 2, D - 2 * (5 * D // 16))
    bufs = (W, WO)
    rows_of = (D // N, F // N)

    def piece(ph, dr, k, c, excl, xb):
        R = rows_of[ph]
        q = R // 4
        row = pl.multiple_of(origin(dr, k) * R + dr * (R // 2) + c * q, q)
        if excl:
            col = pl.multiple_of(xb * (E[ph] + M[ph]), 128)
            return bufs[ph].at[pl.ds(row, q), pl.ds(col, E[ph])]
        return bufs[ph].at[pl.ds(row, q), pl.ds(E[ph], M[ph])]

    def mk(ref, ssem, rsem, dev):
        return pltpu.make_async_remote_copy(
            src_ref=ref, dst_ref=ref, send_sem=ssem, recv_sem=rsem,
            device_id=dev, device_id_type=MESH)

    def dev(seq=None, dp=None):
        return {"seq": s if seq is None else seq, "dp": d if dp is None else dp}

    def ring_desc(ph, dr, k, at, p):
        return mk(piece(ph, dr, at, core, p == 0, x), rs.at[ph, dr, p, k % 2],
                  rr.at[ph, dr, k - 1, p], dev(dp=ring_to[dr]))

    def part_desc(ph, dr, k, c, p):
        return mk(piece(ph, dr, k, c, p == 0, x), ps.at[ph, dr, p, k % 2],
                  pr.at[ph, dr, k - 1, p], dev(seq=partner))

    def x_desc(ph, dr, k, xb):
        return mk(piece(ph, dr, k, core, True, xb), xs.at[ph, dr, k % 2],
                  xr.at[ph, dr, k - 1], dev(seq=xpeer))

    def px_desc(ph, dr, k, c):
        return mk(piece(ph, dr, k, c, True, 1 - x), pxs.at[ph, dr, k % 2],
                  pxr.at[ph, dr, k - 1], dev(seq=partner))

    def send(desc, k):
        @pl.when(k > 2)
        def _():
            desc.wait_send()
        desc.start()

    def relay(ph, k):
        for p in (0, 1):
            for dr in (0, 1):
                ring_desc(ph, dr, k, k, p).wait_recv()

                @pl.when(k < N - 1)
                def _():
                    send(ring_desc(ph, dr, k + 1, k, p), k + 1)
                if p == 0:
                    send(x_desc(ph, dr, k, x), k)
                send(part_desc(ph, dr, k, core, p), k)

    def xrelay(ph, k):
        for dr in (0, 1):
            x_desc(ph, dr, k, 1 - x).wait_recv()
            send(px_desc(ph, dr, k, core), k)

    def collect(ph, k):
        for dr in (0, 1):
            for p in (0, 1):
                part_desc(ph, dr, k, 1 - core, p).wait_recv()
            px_desc(ph, dr, k, 1 - core).wait_recv()

    def drain(ph):
        for k in (N - 2, N - 1):
            for dr in (0, 1):
                for p in (0, 1):
                    ring_desc(ph, dr, k, k, p).wait_send()
                    part_desc(ph, dr, k, core, p).wait_send()
                x_desc(ph, dr, k, x).wait_send()
                px_desc(ph, dr, k, core).wait_send()

    R = D // N
    RO = F // N
    g = F // 4
    base = pl.multiple_of(d * R, R)
    src_dst = (
        (wqkv.at[:, pl.ds(0, F)], 0, F), (wgate.at[:, pl.ds(0, g)], F, g),
        (wqkv.at[:, pl.ds(F, F)], F + g, F), (wgate.at[:, pl.ds(g, 2 * g)], 2 * F + g, 2 * g),
        (wqkv.at[:, pl.ds(2 * F, F)], 2 * F + 3 * g, F),
        (wgate.at[:, pl.ds(3 * g, g)], 3 * F + 3 * g, g),
    )
    loads = [pltpu.make_async_copy(a, W.at[pl.ds(base, R), pl.ds(c0, w)], loc_sem.at[i])
             for i, (a, c0, w) in enumerate(src_dst)]
    loads.append(pltpu.make_async_copy(
        wout, WO.at[pl.ds(pl.multiple_of(d * RO, RO), RO), :], loc_sem.at[6]))
    for c in loads:
        c.start()

    barrier = pltpu.get_barrier_semaphore()
    for who in (dev(dp=ring_to[0]), dev(dp=ring_to[1]), dev(seq=partner), dev(seq=xpeer)):
        pl.semaphore_signal(barrier, inc=1, device_id=who, device_id_type=MESH)

    @pl.when(s > 0)
    def _():
        pl.semaphore_signal(barrier, inc=1, device_id=dev(seq=s - 1), device_id_type=MESH)

    @pl.when(s < n_seq - 1)
    def _():
        pl.semaphore_signal(barrier, inc=1, device_id=dev(seq=s + 1), device_id_type=MESH)
    for c in loads:
        c.wait()
    pl.semaphore_wait(barrier, 4 + jnp.where(s > 0, 1, 0) + jnp.where(s < n_seq - 1, 1, 0))

    for p in (0, 1):
        for dr in (0, 1):
            ring_desc(0, dr, 1, 0, p).start()

    cum = ld[...]
    lane = lax.broadcasted_iota(jnp.int32, (H, T), 1)
    step = 1
    while step < T:
        cum = cum + jnp.where(lane >= step, pltpu.roll(cum, step, 1), 0.0)
        step *= 2
    for h in range(H):
        crow[h] = jnp.broadcast_to(cum[h:h + 1, :], (8, T))
        ccol[h] = jnp.broadcast_to(cum[h:h + 1, :], (hd, T)).T

    tile = F // 2
    tiles = 4 * F // tile
    hr = R // 2

    def chunk(k):
        o = [origin(dr, k) for dr in (0, 1)]
        rows = []
        for dr in (0, 1):
            b = pl.multiple_of(o[dr] * R, R)
            lhs[:, dr * hr:(dr + 1) * hr] = tok[:, pl.ds(b, R)][:, dr * hr:(dr + 1) * hr]
            rows.append(pl.ds(pl.multiple_of(b + dr * hr, hr), hr))

        @pl.loop(0, tiles)
        def _(j):
            cols = pl.ds(pl.multiple_of(j * tile, tile), tile)
            w = jnp.concatenate([W[rows[0], cols], W[rows[1], cols]], axis=0)
            acc[:, cols] += jnp.dot(lhs[...], w, preferred_element_type=F32)

    @pl.loop(0, tiles)
    def _(j):
        cols = pl.ds(pl.multiple_of(j * tile, tile), tile)
        acc[:, cols] = jnp.dot(tok[:, pl.ds(base, R)], W[pl.ds(base, R), cols],
                               preferred_element_type=F32)

    def op(k):
        @pl.when(k <= N - 1)
        def _():
            relay(1, k)

        @pl.when(jnp.logical_and(k >= 2, k <= N))
        def _():
            xrelay(1, k - 1)

    @pl.loop(1, N + 2)
    def _(t):
        @pl.when(t <= N - 1)
        def _():
            relay(0, t)

        @pl.when(t == N - 2)
        def _():
            for p in (0, 1):
                for dr in (0, 1):
                    ring_desc(1, dr, 1, 0, p).start()

        @pl.when(jnp.logical_and(t >= 2, t <= N))
        def _():
            xrelay(0, t - 1)

        @pl.when(t >= N)
        def _():
            op(t - N + 1)

        @pl.when(t >= 3)
        def _():
            collect(0, t - 2)
            chunk(t - 2)

    def silu(v):
        return (v / (1.0 + jnp.exp(-v))).astype(BF16)

    def cols_at(c):
        return pl.ds(pl.multiple_of(c, 128), hd)

    @pl.loop(0, H)
    def _(h):
        kk = silu(acc[:, cols_at(F + g + h * hd)])
        vv = silu(acc[:, cols_at(2 * F + 3 * g + h * hd)])
        k_s[h] = kk
        v_s[h] = vv
        q_s[h] = silu(acc[:, cols_at(h * hd)])
        c = ccol[h]
        sk = (kk.astype(F32) * jnp.exp(c[T - 1:T, :] - c)).astype(BF16)
        st_local[h] = lax.dot_general(sk, vv, (((0,), (0,)), ((), ())),
                                      preferred_element_type=F32)

    def chain_desc(to):
        return pltpu.make_async_remote_copy(
            src_ref=st_send, dst_ref=st_recv, send_sem=ch_s, recv_sem=ch_r,
            device_id=dev(seq=to), device_id_type=MESH)

    @pl.when(s == 0)
    def _():
        st_recv[...] = jnp.zeros_like(st_recv)
        st_send[...] = st_local[...].astype(BF16)
        chain_desc(s + 1).start()

    blk = T // 2
    tri = (lax.broadcasted_iota(jnp.int32, (blk, blk), 1)
           <= lax.broadcasted_iota(jnp.int32, (blk, blk), 0))

    @pl.loop(0, H)
    def _(h):
        op(h + 3)
        for b in (0, 1):
            r = slice(b * blk, (b + 1) * blk)
            q = q_s[h, r, :]
            c = jnp.concatenate([ccol[h, r, :]] * (blk // hd), axis=1)
            total = None
            for e in range(b + 1):
                z = slice(e * blk, (e + 1) * blk)
                sc = lax.dot_general(q, k_s[h, z, :], (((1,), (1,)), ((), ())),
                                     preferred_element_type=F32)
                gap = c - crow[h, 0:1, z]
                if e == b:
                    gap = jnp.where(tri, gap, -1e30)
                w = (sc * jnp.exp(gap)).astype(BF16)
                y = jnp.dot(w, v_s[h, z, :], preferred_element_type=F32)
                total = y if total is None else total + y
            att[h, r, :] = total

        @pl.when(jnp.logical_and(s > 0, h == (s * H) // n_seq))
        def _():
            chain_desc(s).wait_recv()

            @pl.when(s < n_seq - 1)
            def _():
                for j in range(H):
                    keep = jnp.exp(ccol[j, T - 1:T, :])
                    st_send[j] = (keep * st_recv[j].astype(F32) + st_local[j]).astype(BF16)
                chain_desc(s + 1).start()

    if N > H + 2:
        @pl.loop(H + 3, N + 1)
        def _(k):
            op(k)

    ss[...] = jnp.zeros_like(ss)

    @pl.loop(0, H)
    def _(h):
        inter = jnp.dot(q_s[h], st_recv[h], preferred_element_type=F32)
        a = att[h] + inter * jnp.exp(ccol[h])
        att[h] = a
        ss[...] += a * a

    inv = lax.rsqrt(jnp.sum(ss[...], axis=1, keepdims=True) * (1.0 / F) + 1e-06)
    ss[...] = jnp.broadcast_to(inv, ss.shape)

    @pl.loop(0, H)
    def _(h):
        f = h * hd
        gc = jnp.where(f < g, F + f, jnp.where(f < 3 * g, 2 * F + f, 3 * F + f))
        gate = 1.0 / (1.0 + jnp.exp(-acc[:, cols_at(gc)]))
        gated[:, cols_at(f)] = (att[h] * ss[...] * gain[:, cols_at(f)] * gate).astype(BF16)

    @pl.loop(1, N)
    def _(k):
        collect(1, k)

    @pl.loop(0, D // tile)
    def _(j):
        cols = pl.ds(pl.multiple_of(j * tile, tile), tile)
        out[:, cols] = jnp.dot(gated[...], WO[:, cols], preferred_element_type=F32).astype(BF16)

    drain(0)
    drain(1)

    @pl.when(s < n_seq - 1)
    def _():
        chain_desc(s + 1).wait_send()


def body(n_dp, n_seq, tokens, log_decay, w_qkv, w_gate, w_out, norm_gain):
    tok = tokens[0]
    T, D = tok.shape
    H = log_decay.shape[1]
    F = norm_gain.shape[0]
    hd = F // H
    R = D // n_dp
    vm = pl.BlockSpec(memory_space=pltpu.VMEM)
    hbm = pl.BlockSpec(memory_space=pl.ANY)
    dma = pltpu.SemaphoreType.DMA
    n = n_dp - 1
    y = pl.pallas_call(
        functools.partial(fused, n_dp, n_seq),
        out_shape=jax.ShapeDtypeStruct((T, D), BF16),
        in_specs=[vm, vm, vm, hbm, hbm, hbm],
        out_specs=vm,
        scratch_shapes=[
            pltpu.VMEM((D, 4 * F), BF16), pltpu.VMEM((F, D), BF16),
            pltpu.VMEM((T, 4 * F), F32), pltpu.VMEM((T, R), BF16),
            pltpu.VMEM((H, T, hd), BF16), pltpu.VMEM((H, T, hd), BF16),
            pltpu.VMEM((H, T, hd), BF16), pltpu.VMEM((H, T, hd), F32),
            pltpu.VMEM((H, T, hd), F32), pltpu.VMEM((H, 8, T), F32),
            pltpu.VMEM((T, hd), F32), pltpu.VMEM((T, F), BF16),
            pltpu.VMEM((H, hd, hd), F32), pltpu.VMEM((H, hd, hd), BF16),
            pltpu.VMEM((H, hd, hd), BF16),
            dma((7,)),
            dma((2, 2, n, 2)), dma((2, 2, n, 2)), dma((2, 2, n)), dma((2, 2, n)),
            dma((2, 2, 2, 2)), dma((2, 2, 2, 2)), dma((2, 2, 2)), dma((2, 2, 2)),
            dma, dma,
        ],
        compiler_params=pltpu.CompilerParams(
            collective_id=0, has_side_effects=True, vmem_limit_bytes=60 * 1024 * 1024),
    )(tok, log_decay[0], norm_gain[None], w_qkv, w_gate, w_out)
    return y[None]


def solution(mesh):
    placed = (
        P("dp", "seq", None),
        P("dp", None, "seq"),
        P("dp", None),
        P("dp", None),
        P("dp", None),
        P(),
    )
    return jax.shard_map(
        functools.partial(body, mesh.shape["dp"], mesh.shape["seq"]),
        mesh=mesh, in_specs=placed, out_specs=P("dp", "seq", None), check_vma=False
    )
```

```python
import functools

import jax
import jax.numpy as jnp
from jax import lax
from jax.experimental import pallas as pl
from jax.experimental.pallas import tpu as pltpu
from jax.sharding import PartitionSpec as P

MESH = pl.DeviceIdType.MESH
F32 = jnp.float32
BF16 = jnp.bfloat16


def fused(n_dp, n_seq, tok_hbm, ld, gain, wqkv, wgate, wout, out, tok, ob, W, WO, acc, lhs, q_s, k_s, v_s,
          att, ccol, crow, ss, gated, st_local, st_recv, st_send, loc_sem,
          tok_sem, out_sem, rr, pr, xr, pxr, rs, ps, xs, pxs,
          rr1, pr1, xr1, pxr1, rs1, ps1, xs1, pxs1, ch_s, ch_r):
    T, D = tok_hbm.shape
    H = ld.shape[0]
    F = gain.shape[1]
    hd = F // H
    N = n_dp
    s = lax.axis_index("seq")
    d = lax.axis_index("dp")
    core = s % 2
    x = (s // 2) % 2
    partner = s + 1 - 2 * core
    xpeer = s + 2 - 4 * x
    half = N // 2

    def pos_of(i):
        return jnp.where(i % 2 == 0, i // 2, N - 1 - i // 2)

    def dev_at(p):
        p = lax.rem(p + 2 * N, N)
        return jnp.where(p < half, 2 * p, 2 * (N - 1 - p) + 1)

    pos = pos_of(d)
    ring_to = (dev_at(pos + 1), dev_at(pos - 1))

    def origin(dr, k):
        return dev_at(pos - k) if dr == 0 else dev_at(pos + k)

    E = (F + F // 4, 5 * D // 16)
    M = (F + F // 2, D - 2 * (5 * D // 16))
    bufs = (W, WO)
    rows_of = (D // N, F // N)

    sems = ((rr, pr, xr, pxr, rs, ps, xs, pxs), (rr1, pr1, xr1, pxr1, rs1, ps1, xs1, pxs1))

    def slot(ph, k):
        return k % 2 if ph == 0 else k - 1

    def piece(ph, dr, k, c, excl, xb):
        R = rows_of[ph]
        if ph == 0:
            q = R // 4
            row = origin(dr, k) * R + dr * (R // 2) + c * q
        else:
            q = R // 2
            row = origin(dr, k) * R + c * q
        row = pl.multiple_of(row, q)
        if excl:
            col = pl.multiple_of(xb * (E[ph] + M[ph]), 128)
            return bufs[ph].at[pl.ds(row, q), pl.ds(col, E[ph])]
        return bufs[ph].at[pl.ds(row, q), pl.ds(E[ph], M[ph])]

    def mk(ref, ssem, rsem, dev):
        return pltpu.make_async_remote_copy(
            src_ref=ref, dst_ref=ref, send_sem=ssem, recv_sem=rsem,
            device_id=dev, device_id_type=MESH)

    def dev(seq=None, dp=None):
        return {"seq": s if seq is None else seq, "dp": d if dp is None else dp}

    def ring_desc(ph, dr, k, at, p):
        return mk(piece(ph, dr, at, core, p == 0, x), sems[ph][4].at[dr, p, slot(ph, k)],
                  sems[ph][0].at[dr, p, k - 1], dev(dp=ring_to[dr]))

    def part_desc(ph, dr, k, c, p):
        return mk(piece(ph, dr, k, c, p == 0, x), sems[ph][5].at[dr, p, slot(ph, k)],
                  sems[ph][1].at[dr, p, k - 1], dev(seq=partner))

    def x_desc(ph, dr, k, xb):
        return mk(piece(ph, dr, k, core, True, xb), sems[ph][6].at[dr, slot(ph, k)],
                  sems[ph][2].at[dr, k - 1], dev(seq=xpeer))

    def px_desc(ph, dr, k, c):
        return mk(piece(ph, dr, k, c, True, 1 - x), sems[ph][7].at[dr, slot(ph, k)],
                  sems[ph][3].at[dr, k - 1], dev(seq=partner))

    def send(desc, k):
        @pl.when(k > 2)
        def _():
            desc.wait_send()
        desc.start()

    def relay(ph, k):
        for p in (0, 1):
            for dr in (0, 1):
                ring_desc(ph, dr, k, k, p).wait_recv()

                @pl.when(k < N - 1)
                def _():
                    send(ring_desc(ph, dr, k + 1, k, p), k + 1)
                if p == 0:
                    send(x_desc(ph, dr, k, x), k)
                send(part_desc(ph, dr, k, core, p), k)

    def xrelay(ph, k):
        for dr in (0, 1):
            x_desc(ph, dr, k, 1 - x).wait_recv()
            send(px_desc(ph, dr, k, core), k)

    def collect(ph, k):
        for dr in (0, 1):
            for p in (0, 1):
                part_desc(ph, dr, k, 1 - core, p).wait_recv()
            px_desc(ph, dr, k, 1 - core).wait_recv()

    def drain(ph):
        for k in (N - 2, N - 1):
            for dr in (0, 1):
                for p in (0, 1):
                    ring_desc(ph, dr, k, k, p).wait_send()
                    part_desc(ph, dr, k, core, p).wait_send()
                x_desc(ph, dr, k, x).wait_send()
                px_desc(ph, dr, k, core).wait_send()

    K = N // 2

    def has(dr, k, p):
        return k < K or (k == K and p == dr)

    every = [(k, dr, p) for k in range(1, K + 1) for dr in (0, 1) for p in (0, 1) if has(dr, k, p)]

    def op(k):
        for p in (0, 1):
            for dr in (0, 1):
                if not has(dr, k, p):
                    continue
                ring_desc(1, dr, k, k, p).wait_recv()
                if has(dr, k + 1, p):
                    ring_desc(1, dr, k + 1, k, p).start()
                if p == 0:
                    x_desc(1, dr, k, x).start()
                part_desc(1, dr, k, core, p).start()
        for dr in (0, 1):
            if has(dr, k - 1, 0) and k > 1:
                x_desc(1, dr, k - 1, 1 - x).wait_recv()
                px_desc(1, dr, k - 1, core).start()

    def collect1():
        for k, dr, p in every:
            part_desc(1, dr, k, 1 - core, p).wait_recv()
            if p == 0:
                px_desc(1, dr, k, 1 - core).wait_recv()

    def drain1():
        for k, dr, p in every:
            ring_desc(1, dr, k, k, p).wait_send()
            part_desc(1, dr, k, core, p).wait_send()
            if p == 0:
                x_desc(1, dr, k, x).wait_send()
                px_desc(1, dr, k, core).wait_send()

    R = D // N
    RO = F // N
    g = F // 4
    base = pl.multiple_of(d * R, R)
    src_dst = (
        (wqkv.at[:, pl.ds(0, F)], 0, F), (wgate.at[:, pl.ds(0, g)], F, g),
        (wqkv.at[:, pl.ds(F, F)], F + g, F), (wgate.at[:, pl.ds(g, 2 * g)], 2 * F + g, 2 * g),
        (wqkv.at[:, pl.ds(2 * F, F)], 2 * F + 3 * g, F),
        (wgate.at[:, pl.ds(3 * g, g)], 3 * F + 3 * g, g),
    )
    loads = [pltpu.make_async_copy(a, W.at[pl.ds(base, R), pl.ds(c0, w)], loc_sem.at[i])
             for i, (a, c0, w) in enumerate(src_dst)]
    loads.append(pltpu.make_async_copy(
        wout, WO.at[pl.ds(pl.multiple_of(d * RO, RO), RO), :], loc_sem.at[6]))
    for c in loads:
        c.start()
    tok_load = pltpu.make_async_copy(tok_hbm, tok, tok_sem)
    tok_load.start()

    barrier = pltpu.get_barrier_semaphore()
    for who in (dev(dp=ring_to[0]), dev(dp=ring_to[1]), dev(seq=partner), dev(seq=xpeer)):
        pl.semaphore_signal(barrier, inc=1, device_id=who, device_id_type=MESH)

    @pl.when(s > 0)
    def _():
        pl.semaphore_signal(barrier, inc=1, device_id=dev(seq=s - 1), device_id_type=MESH)

    @pl.when(s < n_seq - 1)
    def _():
        pl.semaphore_signal(barrier, inc=1, device_id=dev(seq=s + 1), device_id_type=MESH)
    for c in loads:
        c.wait()
    pl.semaphore_wait(barrier, 4 + jnp.where(s > 0, 1, 0) + jnp.where(s < n_seq - 1, 1, 0))

    for p in (0, 1):
        for dr in (0, 1):
            ring_desc(0, dr, 1, 0, p).start()

    cum = ld[...]
    lane = lax.broadcasted_iota(jnp.int32, (H, T), 1)
    step = 1
    while step < T:
        cum = cum + jnp.where(lane >= step, pltpu.roll(cum, step, 1), 0.0)
        step *= 2
    for h in range(H):
        crow[h] = jnp.broadcast_to(cum[h:h + 1, :], (8, T))
        ccol[h] = jnp.broadcast_to(cum[h:h + 1, :], (hd, T)).T

    tile = F // 2
    tiles = 4 * F // tile
    hr = R // 2

    def chunk(k):
        o = [origin(dr, k) for dr in (0, 1)]
        rows = []
        for dr in (0, 1):
            b = pl.multiple_of(o[dr] * R, R)
            lhs[:, dr * hr:(dr + 1) * hr] = tok[:, pl.ds(b, R)][:, dr * hr:(dr + 1) * hr]
            rows.append(pl.ds(pl.multiple_of(b + dr * hr, hr), hr))

        @pl.loop(0, tiles)
        def _(j):
            cols = pl.ds(pl.multiple_of(j * tile, tile), tile)
            w = jnp.concatenate([W[rows[0], cols], W[rows[1], cols]], axis=0)
            acc[:, cols] += jnp.dot(lhs[...], w, preferred_element_type=F32)

    tok_load.wait()

    @pl.loop(0, tiles)
    def _(j):
        cols = pl.ds(pl.multiple_of(j * tile, tile), tile)
        acc[:, cols] = jnp.dot(tok[:, pl.ds(base, R)], W[pl.ds(base, R), cols],
                               preferred_element_type=F32)

    @pl.loop(1, N + 2)
    def _(t):
        @pl.when(t <= N - 1)
        def _():
            relay(0, t)

        @pl.when(t == N - 2)
        def _():
            for p in (0, 1):
                for dr in (0, 1):
                    ring_desc(1, dr, 1, 0, p).start()

        @pl.when(jnp.logical_and(t >= 2, t <= N))
        def _():
            xrelay(0, t - 1)

        for i in (1, 2):
            @pl.when(t == N + i - 1)
            def _():
                op(i)

        @pl.when(t >= 3)
        def _():
            collect(0, t - 2)
            chunk(t - 2)

    def silu(v):
        return (v / (1.0 + jnp.exp(-v))).astype(BF16)

    def cols_at(c):
        return pl.ds(pl.multiple_of(c, 128), hd)

    @pl.loop(0, H)
    def _(h):
        kk = silu(acc[:, cols_at(F + g + h * hd)])
        vv = silu(acc[:, cols_at(2 * F + 3 * g + h * hd)])
        k_s[h] = kk
        v_s[h] = vv
        q_s[h] = silu(acc[:, cols_at(h * hd)])
        c = ccol[h]
        sk = (kk.astype(F32) * jnp.exp(c[T - 1:T, :] - c)).astype(BF16)
        st_local[h] = lax.dot_general(sk, vv, (((0,), (0,)), ((), ())),
                                      preferred_element_type=F32)

    def chain_desc(to):
        return pltpu.make_async_remote_copy(
            src_ref=st_send, dst_ref=st_recv, send_sem=ch_s, recv_sem=ch_r,
            device_id=dev(seq=to), device_id_type=MESH)

    @pl.when(s == 0)
    def _():
        st_recv[...] = jnp.zeros_like(st_recv)
        st_send[...] = st_local[...].astype(BF16)
        chain_desc(s + 1).start()

    later = list(range(3, K + 1))
    blk = T // 2
    tri = (lax.broadcasted_iota(jnp.int32, (blk, blk), 1)
           <= lax.broadcasted_iota(jnp.int32, (blk, blk), 0))

    @pl.loop(0, H)
    def _(h):
        for i, k in enumerate(later):
            @pl.when(h == (i * H * 3) // (4 * len(later)))
            def _():
                op(k)
        for b in (0, 1):
            r = slice(b * blk, (b + 1) * blk)
            q = q_s[h, r, :]
            c = jnp.concatenate([ccol[h, r, :]] * (blk // hd), axis=1)
            total = None
            for e in range(b + 1):
                z = slice(e * blk, (e + 1) * blk)
                sc = lax.dot_general(q, k_s[h, z, :], (((1,), (1,)), ((), ())),
                                     preferred_element_type=F32)
                gap = c - crow[h, 0:1, z]
                if e == b:
                    gap = jnp.where(tri, gap, -1e30)
                w = (sc * jnp.exp(gap)).astype(BF16)
                y = jnp.dot(w, v_s[h, z, :], preferred_element_type=F32)
                total = y if total is None else total + y
            att[h, r, :] = total

        @pl.when(jnp.logical_and(s > 0, h == (s * H) // n_seq))
        def _():
            chain_desc(s).wait_recv()

            @pl.when(s < n_seq - 1)
            def _():
                for j in range(H):
                    keep = jnp.exp(ccol[j, T - 1:T, :])
                    st_send[j] = (keep * st_recv[j].astype(F32) + st_local[j]).astype(BF16)
                chain_desc(s + 1).start()

    ss[...] = jnp.zeros_like(ss)

    @pl.loop(0, H)
    def _(h):
        inter = jnp.dot(q_s[h], st_recv[h], preferred_element_type=F32)
        a = att[h] + inter * jnp.exp(ccol[h])
        att[h] = a
        ss[...] += a * a

    op(K + 1)
    inv = lax.rsqrt(jnp.sum(ss[...], axis=1, keepdims=True) * (1.0 / F) + 1e-06)
    ss[...] = jnp.broadcast_to(inv, ss.shape)

    @pl.loop(0, H)
    def _(h):
        f = h * hd
        gc = jnp.where(f < g, F + f, jnp.where(f < 3 * g, 2 * F + f, 3 * F + f))
        gate = 1.0 / (1.0 + jnp.exp(-acc[:, cols_at(gc)]))
        gated[:, cols_at(f)] = (att[h] * ss[...] * gain[:, cols_at(f)] * gate).astype(BF16)

    collect1()

    @pl.loop(0, D // tile)
    def _(j):
        cols = pl.ds(pl.multiple_of(j * tile, tile), tile)
        ob[:, cols] = jnp.dot(gated[...], WO[:, cols], preferred_element_type=F32).astype(BF16)
        pltpu.make_async_copy(ob.at[:, cols], out.at[:, cols], out_sem.at[j]).start()

    drain(0)
    drain1()
    for j in range(D // tile):
        cols = pl.ds(j * tile, tile)
        pltpu.make_async_copy(ob.at[:, cols], out.at[:, cols], out_sem.at[j]).wait()

    @pl.when(s < n_seq - 1)
    def _():
        chain_desc(s + 1).wait_send()


def body(n_dp, n_seq, tokens, log_decay, w_qkv, w_gate, w_out, norm_gain):
    tok = tokens[0]
    T, D = tok.shape
    H = log_decay.shape[1]
    F = norm_gain.shape[0]
    hd = F // H
    R = D // n_dp
    vm = pl.BlockSpec(memory_space=pltpu.VMEM)
    hbm = pl.BlockSpec(memory_space=pl.ANY)
    dma = pltpu.SemaphoreType.DMA
    n = n_dp - 1
    m = n_dp // 2
    y = pl.pallas_call(
        functools.partial(fused, n_dp, n_seq),
        out_shape=jax.ShapeDtypeStruct((T, D), BF16),
        in_specs=[hbm, vm, vm, hbm, hbm, hbm],
        out_specs=hbm,
        scratch_shapes=[
            pltpu.VMEM((T, D), BF16), pltpu.VMEM((T, D), BF16),
            pltpu.VMEM((D, 4 * F), BF16), pltpu.VMEM((F, D), BF16),
            pltpu.VMEM((T, 4 * F), F32), pltpu.VMEM((T, R), BF16),
            pltpu.VMEM((H, T, hd), BF16), pltpu.VMEM((H, T, hd), BF16),
            pltpu.VMEM((H, T, hd), BF16), pltpu.VMEM((H, T, hd), F32),
            pltpu.VMEM((H, T, hd), F32), pltpu.VMEM((H, 8, T), F32),
            pltpu.VMEM((T, hd), F32), pltpu.VMEM((T, F), BF16),
            pltpu.VMEM((H, hd, hd), F32), pltpu.VMEM((H, hd, hd), BF16),
            pltpu.VMEM((H, hd, hd), BF16),
            dma((7,)),
            dma, dma((2 * D // F,)),
            dma((2, 2, n)), dma((2, 2, n)), dma((2, n)), dma((2, n)),
            dma((2, 2, 2)), dma((2, 2, 2)), dma((2, 2)), dma((2, 2)),
            dma((2, 2, m)), dma((2, 2, m)), dma((2, m)), dma((2, m)),
            dma((2, 2, m)), dma((2, 2, m)), dma((2, m)), dma((2, m)),
            dma, dma,
        ],
        compiler_params=pltpu.CompilerParams(
            collective_id=0, has_side_effects=True, vmem_limit_bytes=60 * 1024 * 1024),
    )(tok, log_decay[0], norm_gain[None], w_qkv, w_gate, w_out)
    return y[None]


def solution(mesh):
    placed = (
        P("dp", "seq", None),
        P("dp", None, "seq"),
        P("dp", None),
        P("dp", None),
        P("dp", None),
        P(),
    )
    return jax.shard_map(
        functools.partial(body, mesh.shape["dp"], mesh.shape["seq"]),
        mesh=mesh, in_specs=placed, out_specs=P("dp", "seq", None), check_vma=False
    )
```

```python
import functools

import jax
import jax.numpy as jnp
from jax import lax
from jax.experimental import pallas as pl
from jax.experimental.pallas import tpu as pltpu
from jax.sharding import PartitionSpec as P

MESH = pl.DeviceIdType.MESH
F32 = jnp.float32
BF16 = jnp.bfloat16


def fused(n_dp, n_seq, tok_hbm, ld, gain, wqkv, wgate, wout, out, tok, ob, W0, W1, WO, acc0, acc1,
          q_s, k_s, v_s, att, ccol, crow, ss, gated, st_local, st_recv, st_send, loc_sem,
          tok_sem, out_sem, rr, pr, xr, pxr, rs, ps, xs, pxs, ch_s, ch_r):
    T, D = tok_hbm.shape
    H = ld.shape[0]
    F = gain.shape[1]
    hd = F // H
    N = n_dp
    s = lax.axis_index("seq")
    d = lax.axis_index("dp")
    core = s % 2
    x = (s // 2) % 2
    partner = s + 1 - 2 * core
    xpeer = s + 2 - 4 * x
    half = N // 2

    def pos_of(i):
        return jnp.where(i % 2 == 0, i // 2, N - 1 - i // 2)

    def dev_at(p):
        p = lax.rem(p + 2 * N, N)
        return jnp.where(p < half, 2 * p, 2 * (N - 1 - p) + 1)

    pos = pos_of(d)
    ring_to = (dev_at(pos + 1), dev_at(pos - 1))

    def origin(dr, k):
        return dev_at(pos - k) if dr == 0 else dev_at(pos + k)

    cols_all = 2 * F
    E = 5 * cols_all // 16
    M = cols_all - 2 * E
    bufs = (W0, W1, WO)
    rows_of = (D // N, D // N, F // N)

    def piece(ph, dr, k, c, excl, xb):
        q = rows_of[ph] // 2
        row = pl.multiple_of(origin(dr, k) * rows_of[ph] + c * q, q)
        if excl:
            col = pl.multiple_of(xb * (E + M), 128)
            return bufs[ph].at[pl.ds(row, q), pl.ds(col, E)]
        return bufs[ph].at[pl.ds(row, q), pl.ds(E, M)]

    def mk(ref, ssem, rsem, dev):
        return pltpu.make_async_remote_copy(
            src_ref=ref, dst_ref=ref, send_sem=ssem, recv_sem=rsem,
            device_id=dev, device_id_type=MESH)

    def dev(seq=None, dp=None):
        return {"seq": s if seq is None else seq, "dp": d if dp is None else dp}

    def ring_desc(ph, dr, k, at, p):
        return mk(piece(ph, dr, at, core, p == 0, x), rs.at[ph, dr, p, k - 1],
                  rr.at[ph, dr, p, k - 1], dev(dp=ring_to[dr]))

    def part_desc(ph, dr, k, c, p):
        return mk(piece(ph, dr, k, c, p == 0, x), ps.at[ph, dr, p, k - 1],
                  pr.at[ph, dr, p, k - 1], dev(seq=partner))

    def x_desc(ph, dr, k, xb):
        return mk(piece(ph, dr, k, core, True, xb), xs.at[ph, dr, k - 1],
                  xr.at[ph, dr, k - 1], dev(seq=xpeer))

    def px_desc(ph, dr, k, c):
        return mk(piece(ph, dr, k, c, True, 1 - x), pxs.at[ph, dr, k - 1],
                  pxr.at[ph, dr, k - 1], dev(seq=partner))

    K = N // 2

    def has(dr, k, p):
        return k < K or (k == K and p == dr)

    def begin(ph):
        for p in (0, 1):
            for dr in (0, 1):
                if has(dr, 1, p):
                    ring_desc(ph, dr, 1, 0, p).start()

    def relay(ph, k, p):
        for dr in (0, 1):
            if not has(dr, k, p):
                continue
            ring_desc(ph, dr, k, k, p).wait_recv()
            if has(dr, k + 1, p):
                ring_desc(ph, dr, k + 1, k, p).start()
            if p == 0:
                x_desc(ph, dr, k, x).start()
            part_desc(ph, dr, k, core, p).start()

    def xrelay(ph, k):
        for dr in (0, 1):
            if has(dr, k, 0):
                x_desc(ph, dr, k, 1 - x).wait_recv()
                px_desc(ph, dr, k, core).start()

    def collect(ph, k):
        for dr in (0, 1):
            for p in (0, 1):
                if has(dr, k, p):
                    part_desc(ph, dr, k, 1 - core, p).wait_recv()
            if has(dr, k, 0):
                px_desc(ph, dr, k, 1 - core).wait_recv()

    def drain(ph):
        for k in range(1, K + 1):
            for dr in (0, 1):
                for p in (0, 1):
                    if has(dr, k, p):
                        ring_desc(ph, dr, k, k, p).wait_send()
                        part_desc(ph, dr, k, core, p).wait_send()
                if has(dr, k, 0):
                    x_desc(ph, dr, k, x).wait_send()
                    px_desc(ph, dr, k, core).wait_send()

    R = D // N
    RO = F // N
    hw = F // 2
    HG = H // 2
    base = pl.multiple_of(d * R, R)
    g1 = hw // 4
    kq, kk0, kv0 = 0, E, E + M
    gcol = (hw, E + hw, E + hw + g1, E + M + hw)
    src_dst = []
    for gi, buf in ((0, W0), (1, W1)):
        o = gi * hw
        src_dst += [
            (wqkv.at[:, pl.ds(o, hw)], buf, 0, hw),
            (wgate.at[:, pl.ds(o, g1)], buf, gcol[0], g1),
            (wqkv.at[:, pl.ds(F + o, hw)], buf, kk0, hw),
            (wgate.at[:, pl.ds(o + g1, 2 * g1)], buf, gcol[1], 2 * g1),
            (wqkv.at[:, pl.ds(2 * F + o, hw)], buf, kv0, hw),
            (wgate.at[:, pl.ds(o + 3 * g1, g1)], buf, gcol[3], g1),
        ]
    loads = [pltpu.make_async_copy(a, buf.at[pl.ds(base, R), pl.ds(c0, w)], loc_sem.at[i])
             for i, (a, buf, c0, w) in enumerate(src_dst)]
    loads.append(pltpu.make_async_copy(
        wout, WO.at[pl.ds(pl.multiple_of(d * RO, RO), RO), :], loc_sem.at[12]))
    for c in loads:
        c.start()
    tok_load = pltpu.make_async_copy(tok_hbm, tok, tok_sem)
    tok_load.start()

    barrier = pltpu.get_barrier_semaphore()
    for who in (dev(dp=ring_to[0]), dev(dp=ring_to[1]), dev(seq=partner), dev(seq=xpeer)):
        pl.semaphore_signal(barrier, inc=1, device_id=who, device_id_type=MESH)

    @pl.when(s > 0)
    def _():
        pl.semaphore_signal(barrier, inc=1, device_id=dev(seq=s - 1), device_id_type=MESH)

    @pl.when(s < n_seq - 1)
    def _():
        pl.semaphore_signal(barrier, inc=1, device_id=dev(seq=s + 1), device_id_type=MESH)
    for c in loads:
        c.wait()
    pl.semaphore_wait(barrier, 4 + jnp.where(s > 0, 1, 0) + jnp.where(s < n_seq - 1, 1, 0))

    begin(0)

    cum = ld[...]
    lane = lax.broadcasted_iota(jnp.int32, (H, T), 1)
    step = 1
    while step < T:
        cum = cum + jnp.where(lane >= step, pltpu.roll(cum, step, 1), 0.0)
        step *= 2
    for h in range(H):
        crow[h] = jnp.broadcast_to(cum[h:h + 1, :], (8, T))
        ccol[h] = jnp.broadcast_to(cum[h:h + 1, :], (hd, T)).T

    tile = hw
    accs = (acc0, acc1)

    def chunk(gi, o, first=False):
        rows = pl.ds(pl.multiple_of(o * R, R), R)

        @pl.loop(0, cols_all // tile)
        def _(j):
            cols = pl.ds(pl.multiple_of(j * tile, tile), tile)
            y = jnp.dot(tok[:, rows], bufs[gi][rows, cols], preferred_element_type=F32)
            if first:
                accs[gi][:, cols] = y
            else:
                accs[gi][:, cols] += y

    tok_load.wait()
    chunk(0, d, True)
    chunk(1, d, True)

    def silu(v):
        return (v / (1.0 + jnp.exp(-v))).astype(BF16)

    def cols_at(c):
        return pl.ds(pl.multiple_of(c, 128), hd)

    def epilogue(gi):
        a = accs[gi]

        @pl.loop(0, HG)
        def _(i):
            h = gi * HG + i
            kk = silu(a[:, cols_at(kk0 + i * hd)])
            vv = silu(a[:, cols_at(kv0 + i * hd)])
            k_s[h] = kk
            v_s[h] = vv
            q_s[h] = silu(a[:, cols_at(i * hd)])
            c = ccol[h]
            sk = (kk.astype(F32) * jnp.exp(c[T - 1:T, :] - c)).astype(BF16)
            st_local[h] = lax.dot_general(sk, vv, (((0,), (0,)), ((), ())),
                                          preferred_element_type=F32)

        @pl.when(s == 0)
        def _():
            for i in range(gi * HG, (gi + 1) * HG):
                st_recv[i] = jnp.zeros((hd, hd), BF16)
                st_send[i] = st_local[i].astype(BF16)
            chain_desc(gi, s + 1).start()

    def chain_desc(gi, to):
        part = pl.ds(gi * HG, HG)
        return pltpu.make_async_remote_copy(
            src_ref=st_send.at[part], dst_ref=st_recv.at[part], send_sem=ch_s.at[gi],
            recv_sem=ch_r.at[gi], device_id=dev(seq=to), device_id_type=MESH)

    blk = T // 2
    tri = (lax.broadcasted_iota(jnp.int32, (blk, blk), 1)
           <= lax.broadcasted_iota(jnp.int32, (blk, blk), 0))

    def attend(h):
        for b in (0, 1):
            r = slice(b * blk, (b + 1) * blk)
            q = q_s[h, r, :]
            c = jnp.concatenate([ccol[h, r, :]] * (blk // hd), axis=1)
            total = None
            for e in range(b + 1):
                z = slice(e * blk, (e + 1) * blk)
                sc = lax.dot_general(q, k_s[h, z, :], (((1,), (1,)), ((), ())),
                                     preferred_element_type=F32)
                gap = c - crow[h, 0:1, z]
                if e == b:
                    gap = jnp.where(tri, gap, -1e30)
                w = (sc * jnp.exp(gap)).astype(BF16)
                y = jnp.dot(w, v_s[h, z, :], preferred_element_type=F32)
                total = y if total is None else total + y
            att[h, r, :] = total

    def attend_range(lo, hi):
        @pl.loop(lo, hi)
        def _(h):
            attend(h)

    def chain(gi, mine):
        @pl.when(jnp.logical_and(s > 0, mine))
        def _():
            chain_desc(gi, s).wait_recv()

            @pl.when(s < n_seq - 1)
            def _():
                for j in range(gi * HG, (gi + 1) * HG):
                    keep = jnp.exp(ccol[j, T - 1:T, :])
                    st_send[j] = (keep * st_recv[j].astype(F32) + st_local[j]).astype(BF16)
                chain_desc(gi, s + 1).start()

    def grow(gi, k, dr):
        if dr == 0:
            collect(gi, k)
        if k < K or dr == 0:
            chunk(gi, origin(dr, k))

    slots = [(ph, k) for ph in (0, 1, 2) for k in range(1, K + 1)]
    mid = HG // 2
    for i, (ph, k) in enumerate(slots):
        relay(ph, k, 0)
        if i >= 2 and slots[i - 2][0] < 2:
            grow(*slots[i - 2], 0)
        if ph == 2 and k == 3:
            epilogue(1)
        if ph == 1 and k == 3:
            epilogue(0)
        if ph == 1 and k == K:
            attend_range(mid, HG)
        if ph == 2 and k == K:
            chain(1, s < n_seq // 2)
            attend_range(HG, HG + mid)
        relay(ph, k, 1)
        if k == K - 1 and ph < 2:
            begin(ph + 1)
        if i >= 1:
            xrelay(*slots[i - 1])
        if i >= 2 and slots[i - 2][0] < 2:
            grow(*slots[i - 2], 1)
        if ph == 1 and k == 3:
            attend_range(0, mid)
        if ph == 1 and k == K:
            chain(0, s < n_seq // 2)
        if ph == 2 and k == 1:
            chain(0, s >= n_seq // 2)
    attend_range(HG + mid, H)
    chain(1, s >= n_seq // 2)
    xrelay(2, K)

    ss[...] = jnp.zeros_like(ss)

    @pl.loop(0, H)
    def _(h):
        inter = jnp.dot(q_s[h], st_recv[h], preferred_element_type=F32)
        a = att[h] + inter * jnp.exp(ccol[h])
        att[h] = a
        ss[...] += a * a

    inv = lax.rsqrt(jnp.sum(ss[...], axis=1, keepdims=True) * (1.0 / F) + 1e-06)
    ss[...] = jnp.broadcast_to(inv, ss.shape)

    for h in range(H):
        i = h % HG
        gate = 1.0 / (1.0 + jnp.exp(-accs[h // HG][:, gcol[i]:gcol[i] + hd]))
        f = slice(h * hd, (h + 1) * hd)
        gated[:, f] = (att[h] * ss[...] * gain[:, f] * gate).astype(BF16)

    for k in range(1, K + 1):
        collect(2, k)

    @pl.loop(0, D // tile)
    def _(j):
        cols = pl.ds(pl.multiple_of(j * tile, tile), tile)
        ob[:, cols] = jnp.dot(gated[...], WO[:, cols], preferred_element_type=F32).astype(BF16)
        pltpu.make_async_copy(ob.at[:, cols], out.at[:, cols], out_sem.at[j]).start()

    for ph in (0, 1, 2):
        drain(ph)
    for j in range(D // tile):
        cols = pl.ds(j * tile, tile)
        pltpu.make_async_copy(ob.at[:, cols], out.at[:, cols], out_sem.at[j]).wait()

    @pl.when(s < n_seq - 1)
    def _():
        chain_desc(0, s + 1).wait_send()
        chain_desc(1, s + 1).wait_send()


def body(n_dp, n_seq, tokens, log_decay, w_qkv, w_gate, w_out, norm_gain):
    tok = tokens[0]
    T, D = tok.shape
    H = log_decay.shape[1]
    F = norm_gain.shape[0]
    hd = F // H
    vm = pl.BlockSpec(memory_space=pltpu.VMEM)
    hbm = pl.BlockSpec(memory_space=pl.ANY)
    dma = pltpu.SemaphoreType.DMA
    m = n_dp // 2
    y = pl.pallas_call(
        functools.partial(fused, n_dp, n_seq),
        out_shape=jax.ShapeDtypeStruct((T, D), BF16),
        in_specs=[hbm, vm, vm, hbm, hbm, hbm],
        out_specs=hbm,
        scratch_shapes=[
            pltpu.VMEM((T, D), BF16), pltpu.VMEM((T, D), BF16),
            pltpu.VMEM((D, 2 * F), BF16), pltpu.VMEM((D, 2 * F), BF16), pltpu.VMEM((F, D), BF16),
            pltpu.VMEM((T, 2 * F), F32), pltpu.VMEM((T, 2 * F), F32),
            pltpu.VMEM((H, T, hd), BF16), pltpu.VMEM((H, T, hd), BF16),
            pltpu.VMEM((H, T, hd), BF16), pltpu.VMEM((H, T, hd), F32),
            pltpu.VMEM((H, T, hd), F32), pltpu.VMEM((H, 8, T), F32),
            pltpu.VMEM((T, hd), F32), pltpu.VMEM((T, F), BF16),
            pltpu.VMEM((H, hd, hd), F32), pltpu.VMEM((H, hd, hd), BF16),
            pltpu.VMEM((H, hd, hd), BF16),
            dma((13,)), dma, dma((2 * D // F,)),
            dma((3, 2, 2, m)), dma((3, 2, 2, m)), dma((3, 2, m)), dma((3, 2, m)),
            dma((3, 2, 2, m)), dma((3, 2, 2, m)), dma((3, 2, m)), dma((3, 2, m)),
            dma((2,)), dma((2,)),
        ],
        compiler_params=pltpu.CompilerParams(
            collective_id=0, has_side_effects=True, vmem_limit_bytes=60 * 1024 * 1024),
    )(tok, log_decay[0], norm_gain[None], w_qkv, w_gate, w_out)
    return y[None]


def solution(mesh):
    placed = (
        P("dp", "seq", None),
        P("dp", None, "seq"),
        P("dp", None),
        P("dp", None),
        P("dp", None),
        P(),
    )
    return jax.shard_map(
        functools.partial(body, mesh.shape["dp"], mesh.shape["seq"]),
        mesh=mesh, in_specs=placed, out_specs=P("dp", "seq", None), check_vma=False
    )
```

```python
import functools

import jax
import jax.numpy as jnp
from jax import lax
from jax.experimental import pallas as pl
from jax.experimental.pallas import tpu as pltpu
from jax.sharding import PartitionSpec as P

MESH = pl.DeviceIdType.MESH
F32 = jnp.float32
BF16 = jnp.bfloat16


def fused(n_dp, n_seq, tok_hbm, ld, gain, wqkv, wgate, wout, out, tok, ob, W0, W1, WO, acc0, acc1,
          q_s, k_s, v_s, att, ccol, crow, ss, gated, st_local, st_recv, st_send, loc_sem,
          tok_sem, out_sem, rr, pr, xr, pxr, rs, ps, xs, pxs, ch_s, ch_r):
    T, D = tok_hbm.shape
    H = ld.shape[0]
    F = gain.shape[1]
    hd = F // H
    N = n_dp
    s = lax.axis_index("seq")
    d = lax.axis_index("dp")
    core = s % 2
    x = (s // 2) % 2
    partner = s + 1 - 2 * core
    xpeer = s + 2 - 4 * x
    half = N // 2

    def pos_of(i):
        return jnp.where(i % 2 == 0, i // 2, N - 1 - i // 2)

    def dev_at(p):
        p = lax.rem(p + 2 * N, N)
        return jnp.where(p < half, 2 * p, 2 * (N - 1 - p) + 1)

    pos = pos_of(d)
    ring_to = (dev_at(pos + 1), dev_at(pos - 1))

    def origin(dr, k):
        return dev_at(pos - k) if dr == 0 else dev_at(pos + k)

    cols_all = 2 * F
    E = 5 * cols_all // 16
    M = cols_all - 2 * E
    bufs = (W0, W1, WO)
    rows_of = (D // N, D // N, F // N)

    def piece(ph, dr, k, c, excl, xb):
        q = rows_of[ph] // 2
        row = pl.multiple_of(origin(dr, k) * rows_of[ph] + c * q, q)
        if excl:
            col = pl.multiple_of(xb * (E + M), 128)
            return bufs[ph].at[pl.ds(row, q), pl.ds(col, E)]
        return bufs[ph].at[pl.ds(row, q), pl.ds(E, M)]

    def mk(ref, ssem, rsem, dev):
        return pltpu.make_async_remote_copy(
            src_ref=ref, dst_ref=ref, send_sem=ssem, recv_sem=rsem,
            device_id=dev, device_id_type=MESH)

    def dev(seq=None, dp=None):
        return {"seq": s if seq is None else seq, "dp": d if dp is None else dp}

    def ring_desc(ph, dr, k, at, p):
        return mk(piece(ph, dr, at, core, p == 0, x), rs.at[ph, dr, p, k - 1],
                  rr.at[ph, dr, p, k - 1], dev(dp=ring_to[dr]))

    def part_desc(ph, dr, k, c, p):
        return mk(piece(ph, dr, k, c, p == 0, x), ps.at[ph, dr, p, k - 1],
                  pr.at[ph, dr, p, k - 1], dev(seq=partner))

    def x_desc(ph, dr, k, xb):
        return mk(piece(ph, dr, k, core, True, xb), xs.at[ph, dr, k - 1],
                  xr.at[ph, dr, k - 1], dev(seq=xpeer))

    def px_desc(ph, dr, k, c):
        return mk(piece(ph, dr, k, c, True, 1 - x), pxs.at[ph, dr, k - 1],
                  pxr.at[ph, dr, k - 1], dev(seq=partner))

    K = N // 2

    def has(dr, k, p):
        return k < K or (k == K and p == dr)

    def begin(ph):
        for p in (0, 1):
            for dr in (0, 1):
                if has(dr, 1, p):
                    ring_desc(ph, dr, 1, 0, p).start()

    def relay(ph, k, p):
        for dr in (0, 1):
            if not has(dr, k, p):
                continue
            ring_desc(ph, dr, k, k, p).wait_recv()
            if has(dr, k + 1, p):
                ring_desc(ph, dr, k + 1, k, p).start()
            if p == 0:
                x_desc(ph, dr, k, x).start()
            part_desc(ph, dr, k, core, p).start()

    def xrelay(ph, k):
        for dr in (0, 1):
            if has(dr, k, 0):
                x_desc(ph, dr, k, 1 - x).wait_recv()
                px_desc(ph, dr, k, core).start()

    def collect(ph, k):
        for dr in (0, 1):
            for p in (0, 1):
                if has(dr, k, p):
                    part_desc(ph, dr, k, 1 - core, p).wait_recv()
            if has(dr, k, 0):
                px_desc(ph, dr, k, 1 - core).wait_recv()

    def drain(ph):
        for k in range(1, K + 1):
            for dr in (0, 1):
                for p in (0, 1):
                    if has(dr, k, p):
                        ring_desc(ph, dr, k, k, p).wait_send()
                        part_desc(ph, dr, k, core, p).wait_send()
                if has(dr, k, 0):
                    x_desc(ph, dr, k, x).wait_send()
                    px_desc(ph, dr, k, core).wait_send()

    R = D // N
    RO = F // N
    hw = F // 2
    HG = H // 2
    base = pl.multiple_of(d * R, R)
    g1 = hw // 4
    kq, kk0, kv0 = 0, E, E + M
    gcol = (hw, E + hw, E + hw + g1, E + M + hw)
    src_dst = []
    for gi, buf in ((0, W0), (1, W1)):
        o = gi * hw
        src_dst += [
            (wqkv.at[:, pl.ds(o, hw)], buf, 0, hw),
            (wgate.at[:, pl.ds(o, g1)], buf, gcol[0], g1),
            (wqkv.at[:, pl.ds(F + o, hw)], buf, kk0, hw),
            (wgate.at[:, pl.ds(o + g1, 2 * g1)], buf, gcol[1], 2 * g1),
            (wqkv.at[:, pl.ds(2 * F + o, hw)], buf, kv0, hw),
            (wgate.at[:, pl.ds(o + 3 * g1, g1)], buf, gcol[3], g1),
        ]
    loads = [pltpu.make_async_copy(a, buf.at[pl.ds(base, R), pl.ds(c0, w)], loc_sem.at[i])
             for i, (a, buf, c0, w) in enumerate(src_dst)]
    loads.append(pltpu.make_async_copy(
        wout, WO.at[pl.ds(pl.multiple_of(d * RO, RO), RO), :], loc_sem.at[12]))
    for c in loads:
        c.start()
    tok_load = pltpu.make_async_copy(tok_hbm, tok, tok_sem)
    tok_load.start()

    barrier = pltpu.get_barrier_semaphore()
    for who in (dev(dp=ring_to[0]), dev(dp=ring_to[1]), dev(seq=partner), dev(seq=xpeer)):
        pl.semaphore_signal(barrier, inc=1, device_id=who, device_id_type=MESH)

    @pl.when(s > 0)
    def _():
        pl.semaphore_signal(barrier, inc=1, device_id=dev(seq=s - 1), device_id_type=MESH)

    @pl.when(s < n_seq - 1)
    def _():
        pl.semaphore_signal(barrier, inc=1, device_id=dev(seq=s + 1), device_id_type=MESH)
    for c in loads:
        c.wait()
    pl.semaphore_wait(barrier, 4 + jnp.where(s > 0, 1, 0) + jnp.where(s < n_seq - 1, 1, 0))

    begin(0)

    cum = ld[...]
    lane = lax.broadcasted_iota(jnp.int32, (H, T), 1)
    step = 1
    while step < T:
        cum = cum + jnp.where(lane >= step, pltpu.roll(cum, step, 1), 0.0)
        step *= 2
    for h in range(H):
        crow[h] = jnp.broadcast_to(cum[h:h + 1, :], (8, T))
        ccol[h] = jnp.broadcast_to(cum[h:h + 1, :], (hd, T)).T

    tile = hw
    accs = (acc0, acc1)

    def chunk(gi, o, first=False):
        rows = pl.ds(pl.multiple_of(o * R, R), R)

        @pl.loop(0, cols_all // tile)
        def _(j):
            cols = pl.ds(pl.multiple_of(j * tile, tile), tile)
            y = jnp.dot(tok[:, rows], bufs[gi][rows, cols], preferred_element_type=F32)
            if first:
                accs[gi][:, cols] = y
            else:
                accs[gi][:, cols] += y

    tok_load.wait()
    chunk(0, d, True)
    chunk(1, d, True)

    def silu(v):
        return (v / (1.0 + jnp.exp(-v))).astype(BF16)

    def cols_at(c):
        return pl.ds(pl.multiple_of(c, 128), hd)

    def epilogue(gi):
        a = accs[gi]

        @pl.loop(0, HG)
        def _(i):
            h = gi * HG + i
            kk = silu(a[:, cols_at(kk0 + i * hd)])
            vv = silu(a[:, cols_at(kv0 + i * hd)])
            k_s[h] = kk
            v_s[h] = vv
            q_s[h] = silu(a[:, cols_at(i * hd)])
            c = ccol[h]
            sk = (kk.astype(F32) * jnp.exp(c[T - 1:T, :] - c)).astype(BF16)
            st_local[h] = lax.dot_general(sk, vv, (((0,), (0,)), ((), ())),
                                          preferred_element_type=F32)

        @pl.when(s == 0)
        def _():
            for i in range(gi * HG, (gi + 1) * HG):
                st_recv[i] = jnp.zeros((hd, hd), BF16)
                st_send[i] = st_local[i].astype(BF16)
            chain_desc(gi, s + 1).start()

    def chain_desc(gi, to):
        part = pl.ds(gi * HG, HG)
        return pltpu.make_async_remote_copy(
            src_ref=st_send.at[part], dst_ref=st_recv.at[part], send_sem=ch_s.at[gi],
            recv_sem=ch_r.at[gi], device_id=dev(seq=to), device_id_type=MESH)

    blk = T // 2
    tri = (lax.broadcasted_iota(jnp.int32, (blk, blk), 1)
           <= lax.broadcasted_iota(jnp.int32, (blk, blk), 0))

    def attend(h):
        for b in (0, 1):
            r = slice(b * blk, (b + 1) * blk)
            q = q_s[h, r, :]
            c = jnp.concatenate([ccol[h, r, :]] * (blk // hd), axis=1)
            total = None
            for e in range(b + 1):
                z = slice(e * blk, (e + 1) * blk)
                sc = lax.dot_general(q, k_s[h, z, :], (((1,), (1,)), ((), ())),
                                     preferred_element_type=F32)
                gap = c - crow[h, 0:1, z]
                if e == b:
                    gap = jnp.where(tri, gap, -1e30)
                w = (sc * jnp.exp(gap)).astype(BF16)
                y = jnp.dot(w, v_s[h, z, :], preferred_element_type=F32)
                total = y if total is None else total + y
            att[h, r, :] = total

    def attend_range(lo, hi):
        @pl.loop(lo, hi)
        def _(h):
            attend(h)

    def chain(gi, mine):
        @pl.when(jnp.logical_and(s > 0, mine))
        def _():
            chain_desc(gi, s).wait_recv()

            @pl.when(s < n_seq - 1)
            def _():
                for j in range(gi * HG, (gi + 1) * HG):
                    keep = jnp.exp(ccol[j, T - 1:T, :])
                    st_send[j] = (keep * st_recv[j].astype(F32) + st_local[j]).astype(BF16)
                chain_desc(gi, s + 1).start()

    def grow(gi, k, dr):
        if dr == 0:
            collect(gi, k)
        if k < K or dr == 0:
            chunk(gi, origin(dr, k))

    slots = [(ph, k) for ph in (0, 1, 2) for k in range(1, K + 1)]
    mid = HG // 2
    for i, (ph, k) in enumerate(slots):
        relay(ph, k, 0)
        if i >= 2 and slots[i - 2][0] < 2:
            grow(*slots[i - 2], 0)
        if ph == 2 and k == 3:
            attend_range(HG, HG + mid)
        if ph == 1 and k == 3:
            epilogue(0)
        if ph == 1 and k == K:
            attend_range(mid, HG)
        if ph == 2 and k == K:
            chain(1, s < n_seq // 2)
            attend_range(HG + mid, H)
        relay(ph, k, 1)
        if k == K - 1 and ph < 2:
            begin(ph + 1)
        if i >= 1:
            xrelay(*slots[i - 1])
        if i >= 2 and slots[i - 2][0] < 2:
            grow(*slots[i - 2], 1)
        if ph == 1 and k == 3:
            attend_range(0, mid)
        if ph == 2 and k == 2:
            epilogue(1)
        if ph == 1 and k == K:
            chain(0, s < n_seq // 2)
        if ph == 2 and k == 1:
            chain(0, s >= n_seq // 2)
    chain(1, s >= n_seq // 2)
    xrelay(2, K)

    ss[...] = jnp.zeros_like(ss)

    @pl.loop(0, H)
    def _(h):
        inter = jnp.dot(q_s[h], st_recv[h], preferred_element_type=F32)
        a = att[h] + inter * jnp.exp(ccol[h])
        att[h] = a
        ss[...] += a * a

    inv = lax.rsqrt(jnp.sum(ss[...], axis=1, keepdims=True) * (1.0 / F) + 1e-06)
    ss[...] = jnp.broadcast_to(inv, ss.shape)

    for h in range(H):
        i = h % HG
        gate = 1.0 / (1.0 + jnp.exp(-accs[h // HG][:, gcol[i]:gcol[i] + hd]))
        f = slice(h * hd, (h + 1) * hd)
        gated[:, f] = (att[h] * ss[...] * gain[:, f] * gate).astype(BF16)

    for k in range(1, K + 1):
        collect(2, k)

    @pl.loop(0, D // tile)
    def _(j):
        cols = pl.ds(pl.multiple_of(j * tile, tile), tile)
        ob[:, cols] = jnp.dot(gated[...], WO[:, cols], preferred_element_type=F32).astype(BF16)
        pltpu.make_async_copy(ob.at[:, cols], out.at[:, cols], out_sem.at[j]).start()

    for ph in (0, 1, 2):
        drain(ph)
    for j in range(D // tile):
        cols = pl.ds(j * tile, tile)
        pltpu.make_async_copy(ob.at[:, cols], out.at[:, cols], out_sem.at[j]).wait()

    @pl.when(s < n_seq - 1)
    def _():
        chain_desc(0, s + 1).wait_send()
        chain_desc(1, s + 1).wait_send()


def body(n_dp, n_seq, tokens, log_decay, w_qkv, w_gate, w_out, norm_gain):
    tok = tokens[0]
    T, D = tok.shape
    H = log_decay.shape[1]
    F = norm_gain.shape[0]
    hd = F // H
    vm = pl.BlockSpec(memory_space=pltpu.VMEM)
    hbm = pl.BlockSpec(memory_space=pl.ANY)
    dma = pltpu.SemaphoreType.DMA
    m = n_dp // 2
    y = pl.pallas_call(
        functools.partial(fused, n_dp, n_seq),
        out_shape=jax.ShapeDtypeStruct((T, D), BF16),
        in_specs=[hbm, vm, vm, hbm, hbm, hbm],
        out_specs=hbm,
        scratch_shapes=[
            pltpu.VMEM((T, D), BF16), pltpu.VMEM((T, D), BF16),
            pltpu.VMEM((D, 2 * F), BF16), pltpu.VMEM((D, 2 * F), BF16), pltpu.VMEM((F, D), BF16),
            pltpu.VMEM((T, 2 * F), F32), pltpu.VMEM((T, 2 * F), F32),
            pltpu.VMEM((H, T, hd), BF16), pltpu.VMEM((H, T, hd), BF16),
            pltpu.VMEM((H, T, hd), BF16), pltpu.VMEM((H, T, hd), F32),
            pltpu.VMEM((H, T, hd), F32), pltpu.VMEM((H, 8, T), F32),
            pltpu.VMEM((T, hd), F32), pltpu.VMEM((T, F), BF16),
            pltpu.VMEM((H, hd, hd), F32), pltpu.VMEM((H, hd, hd), BF16),
            pltpu.VMEM((H, hd, hd), BF16),
            dma((13,)), dma, dma((2 * D // F,)),
            dma((3, 2, 2, m)), dma((3, 2, 2, m)), dma((3, 2, m)), dma((3, 2, m)),
            dma((3, 2, 2, m)), dma((3, 2, 2, m)), dma((3, 2, m)), dma((3, 2, m)),
            dma((2,)), dma((2,)),
        ],
        compiler_params=pltpu.CompilerParams(
            collective_id=0, has_side_effects=True, vmem_limit_bytes=60 * 1024 * 1024),
    )(tok, log_decay[0], norm_gain[None], w_qkv, w_gate, w_out)
    return y[None]


def solution(mesh):
    placed = (
        P("dp", "seq", None),
        P("dp", None, "seq"),
        P("dp", None),
        P("dp", None),
        P("dp", None),
        P(),
    )
    return jax.shard_map(
        functools.partial(body, mesh.shape["dp"], mesh.shape["seq"]),
        mesh=mesh, in_specs=placed, out_specs=P("dp", "seq", None), check_vma=False
    )
```
